32 devices in a mesh: rep: 2 (over y), tm: 8 (over z, x), col: 2 (over core).
Axes of the slice: x: 2, y: 2, z: 4, core: 2. Of those that a mesh axis runs over, the one named last changes fastest.
Arguments:
- diagonal_block_inverse: float32 [32, 512, 512], P(('rep', 'tm'), None, 'col'), parts along dimension 0, may hold values from -0.1 to 4.5, as said below
- step_map: bfloat16 [32, 512, 512], P(('rep', 'tm'), None, 'col'), parts along dimension 0, may hold values from -1.1 to 1.1
- arrow_map: bfloat16 [32, 32, 512], P(('rep', 'tm'), None, 'col'), parts along dimension 0, may hold values from -0.1796875 to 0.1796875
- arrow_cov: float32 [64, 32], P('rep'), parts along dimension 0, may hold values from -0.5 to 2.5, as said below
Outputs:
- blocks: float32 [32, 512, 512], P(('rep', 'tm'), None, 'col'), parts along dimension 0
- cross: float32 [32, 32, 512], P(('rep', 'tm'), None, 'col'), parts along dimension 0
The draws below stay inside these ranges and needn't reach their ends.
There are 2 independent parts, one for each index of `rep`. The reference program is written for one: setup_inputs(seed, part) draws one part's arguments, and reference() takes and returns one part's arrays. A program takes and returns all parts, laid end to end along the dimension named above; each array names one. Nothing has to cross between parts.
Inputs may be any that keep to these rules, and one draw needn't show every extreme that they name: `diagonal_block_inverse`: symmetric in its last two dimensions. `arrow_cov`: symmetric.
All inputs are finite; a program needn't handle non-finite values.
Results may differ from the reference program's by a relative error of at most 0.019.
Values may be sent and summed in bfloat16 or wider, within the bound.
A program may use at most 384 MiB of HBM per device.

```python
import math
import jax
import jax.numpy as jnp
from jax import lax

NODES = 512
FIXED_EFFECTS = 32
TOTAL_TIME_STEPS = 16


def slow_pairs(key):
    share = 0.5
    return jax.random.uniform(jax.random.fold_in(key, 5), (NODES // 2,), jnp.float32) < share


def draw_diagonal_block_inverse(key, part):
    base = jax.random.fold_in(key, 11)
    first = jax.random.fold_in(base, 0)
    second = jax.random.fold_in(base, 1)
    fourth = jax.random.fold_in(base, 3)
    slow = jnp.tile(slow_pairs(key), 2)
    slow_levels = jnp.exp(jax.random.uniform(first, (TOTAL_TIME_STEPS, NODES), jnp.float32, math.log(0.5), math.log(2.0))) / TOTAL_TIME_STEPS
    fast_levels = jnp.exp(jax.random.uniform(fourth, (TOTAL_TIME_STEPS, NODES), jnp.float32, math.log(0.2), math.log(1.0)))
    levels = jnp.where(slow[None, :], slow_levels, fast_levels)
    noise = jax.random.normal(second, (TOTAL_TIME_STEPS, NODES, NODES), jnp.float32) * (0.2 / math.sqrt(NODES))
    mirrored = noise + jnp.swapaxes(noise, 1, 2)
    ident = (lax.broadcasted_iota(jnp.int32, (NODES, NODES), 0) == lax.broadcasted_iota(jnp.int32, (NODES, NODES), 1)).astype(jnp.float32)
    return ident[None] * levels[:, :, None] + 0.02 * mirrored


def draw_step_map(key, part):
    base = jax.random.fold_in(key, 23)
    random_key_list = jax.random.split(base, 6)
    half = NODES // 2
    slow = slow_pairs(key)
    slow_rate = 0.3 ** (1.0 / (2 * TOTAL_TIME_STEPS))
    fast_rate = jnp.exp(jax.random.uniform(random_key_list[1], (half,), jnp.float32, math.log(0.3), math.log(0.8)))
    paired_rate_value = jnp.where(slow, slow_rate, fast_rate)
    sudden_jump = jax.random.uniform(random_key_list[2], (TOTAL_TIME_STEPS, 1), jnp.float32) < 3.0 / TOTAL_TIME_STEPS
    discarded_items = jax.random.uniform(random_key_list[3], (TOTAL_TIME_STEPS, 1), jnp.float32, 0.7, 0.9)
    rate_values = paired_rate_value[None, :] * jnp.where(sudden_jump, discarded_items, 1.0)
    angles = jax.random.uniform(random_key_list[4], (TOTAL_TIME_STEPS, half), jnp.float32, -math.pi, math.pi)
    cosine = jnp.tile(rate_values * jnp.cos(angles), (1, 2))[:, :, None]
    sine = jnp.tile(rate_values * jnp.sin(angles), (1, 2))[:, :, None]
    rows = lax.broadcasted_iota(jnp.int32, (NODES, NODES), 0)
    cols = lax.broadcasted_iota(jnp.int32, (NODES, NODES), 1)
    same_pair = (rows % half == cols % half)[None]
    on_diag = (rows == cols)[None]
    upper_row = (rows < half)[None]
    rotation = jnp.where(on_diag, cosine, jnp.where(same_pair, jnp.where(upper_row, -sine, sine), 0.0))
    noise = jax.random.normal(random_key_list[5], (TOTAL_TIME_STEPS, NODES, NODES), jnp.float32) * (0.08 / math.sqrt(NODES))
    return (rotation + noise).astype(jnp.bfloat16)


def draw_arrow_cov(key, part):
    base = jax.random.fold_in(key, 37)
    first, second = jax.random.split(base, 2)
    levels = jax.random.uniform(first, (FIXED_EFFECTS,), jnp.float32, 1.0, 2.0)
    noise = jax.random.normal(second, (FIXED_EFFECTS, FIXED_EFFECTS), jnp.float32) * 0.05
    ident = (lax.broadcasted_iota(jnp.int32, (FIXED_EFFECTS, FIXED_EFFECTS), 0) == lax.broadcasted_iota(jnp.int32, (FIXED_EFFECTS, FIXED_EFFECTS), 1)).astype(jnp.float32)
    return ident * levels[None, :] + noise + noise.T


def level_of(stream_key, shape, pieces, least, top_value):
    def one(position, shards_of):
        draws = jax.random.uniform(jax.random.fold_in(jax.random.fold_in(stream_key, 6), position), (shards_of,), jnp.float32, least / len(pieces), top_value / len(pieces))
        return jnp.repeat(jnp.exp(draws), shape[position] // shards_of).reshape((-1,) + (1,) * (len(shape) - position - 1))

    gain = one(*pieces[0])
    for cut in pieces[1:]:
        gain = gain * one(*cut)
    return gain


def bell_draw(own_key, extent, deviation, limit, cuts=(), dtype=jnp.bfloat16):
    result = jax.random.normal(own_key, extent, jnp.float32) * deviation
    if len(cuts) > 0:
        result = level_of(own_key, extent, cuts, -0.22, 0.18) * result
    return jnp.clip(result, min=-limit, max=limit).astype(dtype)


def setup_inputs(seed: int = 0, part: int = 0) -> dict:
    key_of = jax.random.split(jax.random.key(seed), 5)
    own_keys = jax.random.split(jax.random.fold_in(key_of[4], part), 5)
    return {
        "diagonal_block_inverse": draw_diagonal_block_inverse(jax.random.fold_in(jax.random.fold_in(key_of[4], part), 71), part),
        "step_map": draw_step_map(jax.random.fold_in(jax.random.fold_in(key_of[4], part), 71), part),
        "arrow_map": bell_draw(own_keys[2], (TOTAL_TIME_STEPS, FIXED_EFFECTS, NODES), 0.03, 0.1796875, ((0, 8), (2, 2))),
        "arrow_cov": draw_arrow_cov(jax.random.fold_in(jax.random.fold_in(key_of[4], part), 71), part),
    }


def product(left, right):
    return jnp.dot(left.astype(jnp.bfloat16), right.astype(jnp.bfloat16), preferred_element_type=jnp.float32)


def reference(diagonal_block_inverse, step_map, arrow_map, arrow_cov):
    def advance(carry, inputs):
        current, cross = carry
        diag_block, coupling, arrow_rows = inputs
        lower = product(cross, coupling) + product(arrow_cov, arrow_rows)
        upper = product(current, coupling) + product(cross.T, arrow_rows)
        fresh = diag_block + product(coupling.T, upper) + product(arrow_rows.T, lower)
        return (fresh, -lower), (fresh, -lower)

    start = (jnp.zeros((NODES, NODES), jnp.float32), jnp.zeros((FIXED_EFFECTS, NODES), jnp.float32))
    final, output_results = lax.scan(advance, start, (diagonal_block_inverse, step_map, arrow_map), reverse=True)
    return output_results[0], output_results[1]
```

```python
import functools
import jax
import jax.numpy as jnp
from jax import lax
from jax.experimental import pallas as pl
from jax.experimental.pallas import tpu as pltpu
from jax.sharding import PartitionSpec as P

MESH = pl.DeviceIdType.MESH
F32 = jnp.float32
BF16 = jnp.bfloat16
G0, G1, DH1, H0, GC, XP, XPF, XG, XGF, M1X, M0X, CH, CHO, YF = range(14)
COPIES = 14


def mm(left, right):
    return jnp.dot(left, right, preferred_element_type=F32)


def mt(left, right):
    return lax.dot_general(left, right, (((0,), (0,)), ((), ())), preferred_element_type=F32)


def kernel(
    d_ref, g_ref, h_ref, a_ref, out_ref, cross_ref,
    g0f, g1f, dh1f, h0f, gk, pk, t0, t1, p1f, g1cf, m1, m0, pm1, pm0, yin, ys, kb,
    send, recv,
):
    rows = g0f.shape[1]
    wide = g0f.shape[2]
    tall = gk.shape[1]
    tm = lax.axis_index("tm")
    c = lax.axis_index("col")
    o = 1 - c
    pairs = lax.axis_size("tm") // 2
    k = tm // 2
    even = tm % 2 == 0
    odd = tm % 2 == 1
    last = k == pairs - 1
    mate = {"col": o}
    across = {"tm": tm + 1 - 2 * (tm % 2)}

    def copy(which, src, dst, device):
        return pltpu.make_async_remote_copy(
            src_ref=src, dst_ref=dst, send_sem=send.at[which], recv_sem=recv.at[which],
            device_id=device, device_id_type=MESH,
        )

    barrier = pltpu.get_barrier_semaphore()

    def greet(device):
        pl.semaphore_signal(barrier, inc=1, device_id=device, device_id_type=MESH)

    greet(mate)
    greet(across)

    @pl.when(even & (k > 0))
    def _():
        greet({"tm": tm - 2})
        greet({"tm": tm - 1})

    @pl.when(even & jnp.logical_not(last))
    def _():
        greet({"tm": tm + 2})

    @pl.when(odd & jnp.logical_not(last))
    def _():
        greet({"tm": tm + 1})

    g0f[c] = g_ref[0]
    g1f[c] = g_ref[1]
    dh1f[c, :rows] = d_ref[1].astype(BF16)
    dh1f[c, rows:] = h_ref[1]
    h0f[c] = h_ref[0]

    before = jnp.where(even & (k > 0), 2, 0)
    after = jnp.where(last, 0, 1)
    pl.semaphore_wait(barrier, 2 + before + after)

    first = [
        copy(DH1, dh1f.at[c], dh1f.at[c], mate),
        copy(G0, g0f.at[c], g0f.at[c], mate),
        copy(G1, g1f.at[c], g1f.at[c], mate),
    ]
    for one in first:
        one.start()
    first[0].wait_recv()

    def times(left, span, right):
        return mm(left[0, span], right[:wide]) + mm(left[1, span], right[wide:])

    body = pl.ds(0, rows)
    foot = pl.ds(rows, tall - rows)
    whole = pl.ds(0, tall)

    own0 = g_ref[0]
    w = times(dh1f, whole, own0)
    wb = w[:rows].astype(BF16)
    kappa = w[rows:] - h_ref[0].astype(F32)
    first[1].wait_recv()
    for j in range(2):
        span = pl.ds(j * wide, wide)
        pm0[span] = d_ref[0, span] + mt(g0f[j], wb)
    pk[:rows] = pm0[...].astype(BF16)
    pk[rows:] = kappa.astype(BF16)

    def out_p():
        return copy(XP, pk, p1f.at[c], across)

    @pl.when(odd)
    def _():
        out_p().start()

    first[2].wait_recv()
    gk[c, :rows] = times(g1f, body, own0).astype(BF16)
    gk[c, rows:] = kappa.astype(BF16)

    def out_g():
        return copy(XG, gk.at[c], g1cf.at[c], across)

    @pl.when(odd)
    def _():
        out_g().start()

    join = copy(GC, gk.at[c], gk.at[c], mate)
    join.start()
    join.wait_recv()
    for j in range(2):
        t0[pl.ds(j * wide, wide), :] = gk[j, :rows].T
        t1[pl.ds(j * wide, wide), :] = g1f[j].T

    def chain_even():
        return copy(CH, ys, yin.at[c], {"tm": tm - 2})

    def chain_odd():
        return copy(CHO, ys, yin.at[c], {"tm": tm - 1})

    def in_y():
        return copy(CH, ys, yin.at[c], across)

    def in_yo():
        return copy(CHO, ys, yin.at[c], across)

    @pl.when(odd)
    def _():
        m0[...] = gk[...]
        m1[:, :rows] = g1f[...]
        m1[:, rows:] = -dh1f[:, rows:]
        pm1[...] = d_ref[1]

    @pl.when(even)
    def _():
        out_p().wait_recv()
        ahead = copy(XPF, p1f.at[c], p1f.at[c], mate)
        ahead.start()
        ahead.wait_recv()
        own = gk[c, :rows]
        w = times(p1f, whole, own)
        wb = w[:rows].astype(BF16)
        kz = (w[rows:] + gk[c, rows:].astype(F32)).astype(BF16)
        m0[c, rows:] = kz
        for j in range(2):
            span = pl.ds(j * wide, wide)
            pm0[span] += mm(t0[span, :], wb)

        @pl.when(last & (k > 0))
        def _():
            ys[:rows] = pm0[...].astype(BF16)
            ys[rows:] = kz
            chain_even().start()
            chain_odd().start()

        w1 = times(p1f, whole, g_ref[1])
        wb1 = w1[:rows].astype(BF16)
        m1[c, rows:] = (-(w1[rows:] + h_ref[1].astype(F32))).astype(BF16)
        for j in range(2):
            span = pl.ds(j * wide, wide)
            pm1[span] = d_ref[1, span] + mm(t1[span, :], wb1)
        out_g().wait_recv()
        ahead_g = copy(XGF, g1cf.at[c], g1cf.at[c], mate)
        ahead_g.start()
        ahead_g.wait_recv()
        m0[c, :rows] = times(g1cf, body, own).astype(BF16)
        m0x = copy(M0X, m0.at[c], m0.at[c], mate)
        m0x.start()
        m1[c, :rows] = times(g1cf, body, g_ref[1]).astype(BF16)
        m1x = copy(M1X, m1.at[c], m1.at[c], mate)
        m1x.start()
        m0x.wait_recv()
        m1x.wait_recv()
        for j in range(2):
            t0[pl.ds(j * wide, wide), :] = m0[j, :rows].T
            t1[pl.ds(j * wide, wide), :] = m1[j, :rows].T
        ahead.wait_send()
        ahead_g.wait_send()
        m0x.wait_send()
        m1x.wait_send()

    @pl.when(odd)
    def _():
        out_p().wait_send()
        out_g().wait_send()

    @pl.when(last)
    def _():
        yin[...] = jnp.zeros_like(yin)

    @pl.when(jnp.logical_not(last))
    def _():
        @pl.when(even)
        def _():
            in_y().wait_recv()

        @pl.when(odd)
        def _():
            in_yo().wait_recv()

        ahead = copy(YF, yin.at[c], yin.at[c], mate)
        ahead.start()
        ahead.wait()

    cov = a_ref[...].astype(BF16)

    def apply(step, sign, m, t, p):
        for j in range(2):
            part = times(yin, foot, m[j, :rows])
            kb[j] = sign * part + m[j, rows:].astype(F32)
        w = times(yin, body, m[c, :rows]).astype(BF16)
        for j in range(2):
            span = pl.ds(j * wide, wide)
            p[span] += mm(t[span, :], w)

    def emit(step, p):
        edge = mm(cov, kb[c].astype(BF16))
        cross_ref[step] = edge
        edge = edge.astype(BF16)
        for j in range(2):
            span = pl.ds(j * wide, wide)
            out_ref[step, span] = p[span] + mt(kb[j].astype(BF16), edge)

    apply(0, 1.0, m0, t0, pm0)

    @pl.when(even & (k > 0) & jnp.logical_not(last))
    def _():
        ys[:rows] = pm0[...].astype(BF16)
        ys[rows:] = kb[c].astype(BF16)
        chain_even().start()
        chain_odd().start()

    emit(0, pm0)
    apply(1, -1.0, m1, t1, pm1)
    emit(1, pm1)
    for one in first:
        one.wait_send()
    join.wait_send()

    @pl.when(even & (k > 0))
    def _():
        chain_even().wait_send()
        chain_odd().wait_send()


def shards(diagonal_block_inverse, step_map, arrow_map, arrow_cov):
    count, nodes, wide = diagonal_block_inverse.shape
    effects = arrow_map.shape[1]
    tall = nodes + effects
    vmem = pl.BlockSpec(memory_space=pltpu.VMEM)
    return pl.pallas_call(
        kernel,
        out_shape=(
            jax.ShapeDtypeStruct((count, nodes, wide), F32),
            jax.ShapeDtypeStruct((count, effects, wide), F32),
        ),
        in_specs=[vmem] * 4,
        out_specs=(vmem, vmem),
        scratch_shapes=[
            pltpu.VMEM((2, nodes, wide), BF16),
            pltpu.VMEM((2, nodes, wide), BF16),
            pltpu.VMEM((2, tall, wide), BF16),
            pltpu.VMEM((2, effects, wide), BF16),
            pltpu.VMEM((2, tall, wide), BF16),
            pltpu.VMEM((tall, wide), BF16),
            pltpu.VMEM((nodes, nodes), BF16),
            pltpu.VMEM((nodes, nodes), BF16),
            pltpu.VMEM((2, tall, wide), BF16),
            pltpu.VMEM((2, tall, wide), BF16),
            pltpu.VMEM((2, tall, wide), BF16),
            pltpu.VMEM((2, tall, wide), BF16),
            pltpu.VMEM((nodes, wide), F32),
            pltpu.VMEM((nodes, wide), F32),
            pltpu.VMEM((2, tall, wide), BF16),
            pltpu.VMEM((tall, wide), BF16),
            pltpu.VMEM((2, effects, wide), F32),
            pltpu.SemaphoreType.DMA((COPIES,)),
            pltpu.SemaphoreType.DMA((COPIES,)),
        ],
        compiler_params=pltpu.CompilerParams(
            collective_id=0, has_side_effects=True, vmem_limit_bytes=48 * 1024 * 1024
        ),
    )(diagonal_block_inverse, step_map, arrow_map, arrow_cov)


def solution(mesh):
    return jax.shard_map(
        shards,
        mesh=mesh,
        in_specs=(
            P(("rep", "tm"), None, "col"),
            P(("rep", "tm"), None, "col"),
            P(("rep", "tm"), None, "col"),
            P("rep", None),
        ),
        out_specs=(P(("rep", "tm"), None, "col"), P(("rep", "tm"), None, "col")),
        check_vma=False,
    )
```

```python
import functools
import jax
import jax.numpy as jnp
from jax import lax
from jax.experimental import pallas as pl
from jax.experimental.pallas import tpu as pltpu
from jax.sharding import PartitionSpec as P

MESH = pl.DeviceIdType.MESH
F32 = jnp.float32
BF16 = jnp.bfloat16
G0, G1, DH1, GC, XA, XB, XFA, XFB, XG, XGF, M1X, M0X, YA, YB, OA, OB, FA, FB = range(18)
COPIES = 18


def mm(left, right):
    return jnp.dot(left, right, preferred_element_type=F32)


def mt(left, right):
    return lax.dot_general(left, right, (((0,), (0,)), ((), ())), preferred_element_type=F32)


def kernel(
    d_hbm, g_hbm, h_hbm, a_hbm, out_ref, cross_ref,
    d_ref, h_ref, a_ref, g0f, g1f, dh1f, gk, t0, t1, zs, zp, zy, p1f, g1cf, m1, m0, pm1, pm0,
    yin, kb, send, recv, load,
):
    rows = g0f.shape[1]
    wide = g0f.shape[2]
    tall = gk.shape[1]
    half = wide // 2
    early = 3 * half
    edge_rows = tall - rows
    tm = lax.axis_index("tm")
    c = lax.axis_index("col")
    o = 1 - c
    pairs = lax.axis_size("tm") // 2
    k = tm // 2
    even = tm % 2 == 0
    odd = tm % 2 == 1
    last = k == pairs - 1
    mate = {"col": o}
    across = {"tm": tm + 1 - 2 * (tm % 2)}

    def copy(which, src, dst, device):
        return pltpu.make_async_remote_copy(
            src_ref=src, dst_ref=dst, send_sem=send.at[which], recv_sem=recv.at[which],
            device_id=device, device_id_type=MESH,
        )

    loads = [
        pltpu.make_async_copy(d_hbm.at[1], d_ref.at[1], load.at[0]),
        pltpu.make_async_copy(h_hbm, h_ref, load.at[1]),
        pltpu.make_async_copy(g_hbm.at[0], g0f.at[c], load.at[2]),
        pltpu.make_async_copy(g_hbm.at[1], g1f.at[c], load.at[3]),
        pltpu.make_async_copy(d_hbm.at[0], d_ref.at[0], load.at[4]),
        pltpu.make_async_copy(a_hbm, a_ref, load.at[5]),
    ]
    for one in loads:
        one.start()

    barrier = pltpu.get_barrier_semaphore()

    def greet(device):
        pl.semaphore_signal(barrier, inc=1, device_id=device, device_id_type=MESH)

    greet(mate)
    greet(across)

    @pl.when(even & (k > 0))
    def _():
        greet({"tm": tm - 2})

    @pl.when(even & jnp.logical_not(last))
    def _():
        greet({"tm": tm + 2})

    loads[0].wait()
    loads[1].wait()
    dh1f[c, :rows] = d_ref[1].astype(BF16)
    dh1f[c, rows:] = h_ref[1]

    before = jnp.where(even & (k > 0), 1, 0)
    after = jnp.where(even & jnp.logical_not(last), 1, 0)
    pl.semaphore_wait(barrier, 2 + before + after)

    first = [
        copy(DH1, dh1f.at[c], dh1f.at[c], mate),
        copy(G0, g_hbm.at[0], g0f.at[c], mate),
        copy(G1, g_hbm.at[1], g1f.at[c], mate),
    ]
    for one in first:
        one.start()
    for one in loads[2:]:
        one.wait()
    first[0].wait_recv()

    def times(left, span, right):
        return mm(jnp.concatenate([left[0, span], left[1, span]], axis=1), right)

    body = pl.ds(0, rows)
    whole = pl.ds(0, tall)

    def pack(p, edge):
        r = pl.multiple_of(c * wide, wide)
        zs[:half] = p[pl.ds(r, half), :half].astype(BF16)
        zs[half : 2 * half] = p[pl.ds(r + half, half), half:].astype(BF16)
        zs[2 * half : early] = p[pl.ds(r, half), half:].astype(BF16)

        @pl.when(c == 0)
        def _():
            zs[early : 4 * half] = p[wide : wide + half, :half].astype(BF16)
            zs[4 * half : 5 * half] = p[wide + half :, :half].astype(BF16)

        @pl.when(c == 1)
        def _():
            zs[early : 4 * half] = p[half:wide, :half].astype(BF16)
            zs[4 * half : 5 * half] = p[half:wide, half:].astype(BF16)

        zs[5 * half : 5 * half + edge_rows] = edge[:, :half].astype(BF16)
        zs[5 * half + edge_rows :] = edge[:, half:].astype(BF16)

    def unpack(z, full):
        for j in range(2):
            base = j * wide
            lo = pl.ds(base, half)
            hi = pl.ds(base + half, half)
            full[lo, lo] = z[j, :half]
            full[hi, hi] = z[j, half : 2 * half]
            inner = z[j, 2 * half : early]
            full[lo, hi] = inner
            full[hi, lo] = inner.T
            for n in range(2):
                outer = z[j, early + n * half : early + (n + 1) * half]
                far = pl.ds(wide + n * half, half)
                near = pl.ds(j * half, half)
                if j == 0:
                    full[far, near] = outer
                    full[near, far] = outer.T
                else:
                    full[near, far] = outer
                    full[far, near] = outer.T
                full[rows:, pl.ds(base + n * half, half)] = z[
                    j, 5 * half + n * edge_rows : 5 * half + (n + 1) * edge_rows
                ]

    top = pl.ds(0, early)
    low = pl.ds(early, zs.shape[0] - early)

    def pieces(ids, src, dst, device):
        return [
            copy(ids[0], src.at[top], dst.at[top], device),
            copy(ids[1], src.at[low], dst.at[low], device),
        ]

    own0 = g0f[c]
    w = times(dh1f, whole, own0)
    wb = w[:rows].astype(BF16)
    kappa = w[rows:] - h_ref[0].astype(F32)
    first[1].wait_recv()
    for j in range(2):
        span = pl.ds(j * wide, wide)
        pm0[span] = d_ref[0, span] + mt(g0f[j], wb)

    out_p = pieces((XA, XB), zs, zp.at[c], across)

    @pl.when(odd)
    def _():
        pack(pm0, kappa)
        for one in out_p:
            one.start()

    first[2].wait_recv()
    gk[c, :rows] = times(g1f, body, own0).astype(BF16)
    gk[c, rows:] = kappa.astype(BF16)
    out_g = copy(XG, gk.at[c], g1cf.at[c], across)

    @pl.when(odd)
    def _():
        out_g.start()

    join = copy(GC, gk.at[c], gk.at[c], mate)
    join.start()
    join.wait_recv()
    for j in range(2):
        t0[pl.ds(j * wide, wide), :] = gk[j, :rows].T
        t1[pl.ds(j * wide, wide), :] = g1f[j].T

    chain = pieces((YA, YB), zs, zy.at[c], {"tm": tm - 2})

    @pl.when(odd)
    def _():
        m0[...] = gk[...]
        m1[:, :rows] = g1f[...]
        m1[:, rows:] = -dh1f[:, rows:]
        pm1[...] = d_ref[1]

    @pl.when(even)
    def _():
        ahead = pieces((XFA, XFB), zp.at[c], zp.at[c], mate)
        for one, two in zip(out_p, ahead):
            one.wait_recv()
            two.start()
        for two in ahead:
            two.wait_recv()
        unpack(zp, p1f)
        own = gk[c, :rows]
        w = mm(p1f[...], own)
        wb = w[:rows].astype(BF16)
        kz = w[rows:] + gk[c, rows:].astype(F32)
        m0[c, rows:] = kz.astype(BF16)
        for j in range(2):
            span = pl.ds(j * wide, wide)
            pm0[span] += mm(t0[span, :], wb)

        @pl.when(last & (k > 0))
        def _():
            pack(pm0, kz)
            for one in chain:
                one.start()

        w1 = mm(p1f[...], g1f[c])
        wb1 = w1[:rows].astype(BF16)
        m1[c, rows:] = (-(w1[rows:] + h_ref[1].astype(F32))).astype(BF16)
        for j in range(2):
            span = pl.ds(j * wide, wide)
            pm1[span] = d_ref[1, span] + mm(t1[span, :], wb1)
        out_g.wait_recv()
        ahead_g = copy(XGF, g1cf.at[c], g1cf.at[c], mate)
        ahead_g.start()
        ahead_g.wait_recv()
        m0[c, :rows] = times(g1cf, body, own).astype(BF16)
        m0x = copy(M0X, m0.at[c], m0.at[c], mate)
        m0x.start()
        m1[c, :rows] = times(g1cf, body, g1f[c]).astype(BF16)
        m1x = copy(M1X, m1.at[c], m1.at[c], mate)
        m1x.start()
        m0x.wait_recv()
        m1x.wait_recv()
        for j in range(2):
            t0[pl.ds(j * wide, wide), :] = m0[j, :rows].T
            t1[pl.ds(j * wide, wide), :] = m1[j, :rows].T
        for two in ahead:
            two.wait_send()
        ahead_g.wait_send()
        m0x.wait_send()
        m1x.wait_send()

    @pl.when(odd)
    def _():
        for one in out_p:
            one.wait_send()
        out_g.wait_send()

    beside = pieces((OA, OB), zy.at[c], zy.at[c], across)
    inner = pieces((FA, FB), zy.at[c], zy.at[c], mate)

    @pl.when(last)
    def _():
        yin[...] = jnp.zeros_like(yin)

    @pl.when(jnp.logical_not(last))
    def _():
        @pl.when(even)
        def _():
            for n in range(2):
                chain[n].wait_recv()
                inner[n].start()
                beside[n].start()

        @pl.when(odd)
        def _():
            for n in range(2):
                beside[n].wait_recv()
                inner[n].start()

        for one in inner:
            one.wait_recv()
        unpack(zy, yin)

    cov = a_ref[...].astype(BF16)

    def edges(sign, m):
        for j in range(2):
            kb[j] = sign * mm(yin[rows:], m[j, :rows]) + m[j, rows:].astype(F32)

    def apply(m, t, p):
        w = mm(yin[:rows], m[c, :rows]).astype(BF16)
        for j in range(2):
            span = pl.ds(j * wide, wide)
            p[span] += mm(t[span, :], w)

    def emit(step, p):
        edge = mm(cov, kb[c].astype(BF16))
        cross_ref[step] = edge
        edge = edge.astype(BF16)
        for j in range(2):
            span = pl.ds(j * wide, wide)
            out_ref[step, span] = p[span] + mt(kb[j].astype(BF16), edge)

    edges(1.0, m0)
    apply(m0, t0, pm0)

    @pl.when(even & (k > 0) & jnp.logical_not(last))
    def _():
        pack(pm0, kb[c])
        for one in chain:
            one.start()

    emit(0, pm0)
    edges(-1.0, m1)
    apply(m1, t1, pm1)
    emit(1, pm1)
    for one in first:
        one.wait_send()
    join.wait_send()

    @pl.when(jnp.logical_not(last))
    def _():
        for one in inner:
            one.wait_send()

    @pl.when(even & jnp.logical_not(last))
    def _():
        for one in beside:
            one.wait_send()

    @pl.when(even & (k > 0))
    def _():
        for one in chain:
            one.wait_send()


def shards(diagonal_block_inverse, step_map, arrow_map, arrow_cov):
    count, nodes, wide = diagonal_block_inverse.shape
    effects = arrow_map.shape[1]
    tall = nodes + effects
    packed = 5 * (wide // 2) + 2 * effects
    vmem = pl.BlockSpec(memory_space=pltpu.VMEM)
    return pl.pallas_call(
        kernel,
        out_shape=(
            jax.ShapeDtypeStruct((count, nodes, wide), F32),
            jax.ShapeDtypeStruct((count, effects, wide), F32),
        ),
        in_specs=[pl.BlockSpec(memory_space=pl.ANY)] * 4,
        out_specs=(vmem, vmem),
        scratch_shapes=[
            pltpu.VMEM((count, nodes, wide), F32),
            pltpu.VMEM((count, effects, wide), BF16),
            pltpu.VMEM((effects, effects), F32),
            pltpu.VMEM((2, nodes, wide), BF16),
            pltpu.VMEM((2, nodes, wide), BF16),
            pltpu.VMEM((2, tall, wide), BF16),
            pltpu.VMEM((2, tall, wide), BF16),
            pltpu.VMEM((nodes, nodes), BF16),
            pltpu.VMEM((nodes, nodes), BF16),
            pltpu.VMEM((packed, wide // 2), BF16),
            pltpu.VMEM((2, packed, wide // 2), BF16),
            pltpu.VMEM((2, packed, wide // 2), BF16),
            pltpu.VMEM((tall, nodes), BF16),
            pltpu.VMEM((2, tall, wide), BF16),
            pltpu.VMEM((2, tall, wide), BF16),
            pltpu.VMEM((2, tall, wide), BF16),
            pltpu.VMEM((nodes, wide), F32),
            pltpu.VMEM((nodes, wide), F32),
            pltpu.VMEM((tall, nodes), BF16),
            pltpu.VMEM((2, effects, wide), F32),
            pltpu.SemaphoreType.DMA((COPIES,)),
            pltpu.SemaphoreType.DMA((COPIES,)),
            pltpu.SemaphoreType.DMA((6,)),
        ],
        compiler_params=pltpu.CompilerParams(
            collective_id=0, has_side_effects=True, vmem_limit_bytes=48 * 1024 * 1024
        ),
    )(diagonal_block_inverse, step_map, arrow_map, arrow_cov)


def solution(mesh):
    return jax.shard_map(
        shards,
        mesh=mesh,
        in_specs=(
            P(("rep", "tm"), None, "col"),
            P(("rep", "tm"), None, "col"),
            P(("rep", "tm"), None, "col"),
            P("rep", None),
        ),
        out_specs=(P(("rep", "tm"), None, "col"), P(("rep", "tm"), None, "col")),
        check_vma=False,
    )
```

```python
import functools
import jax
import jax.numpy as jnp
from jax import lax
from jax.experimental import pallas as pl
from jax.experimental.pallas import tpu as pltpu
from jax.sharding import PartitionSpec as P

MESH = pl.DeviceIdType.MESH
F32 = jnp.float32
BF16 = jnp.bfloat16
G0, G1, DH1, GC, XA, XB, XFA, XFB, XG, XGF, M1X, M0X, YA, YB, OA, OB, FA, FB = range(18)
COPIES = 18


def mm(left, right):
    return jnp.dot(left, right, preferred_element_type=F32)


def mt(left, right):
    return lax.dot_general(left, right, (((0,), (0,)), ((), ())), preferred_element_type=F32)


def kernel(
    d_hbm, g_hbm, h_hbm, a_hbm, out_ref, cross_ref,
    d_ref, h_ref, a_ref, g0f, g1f, dh1f, gk, t0, t1, zs, zp, zy, p1f, g1cf, m1, m0, pm1, pm0,
    yin, kb, send, recv, load,
):
    rows = g0f.shape[1]
    wide = g0f.shape[2]
    tall = gk.shape[1]
    half = wide // 2
    early = 3 * half
    edge_rows = tall - rows
    tm = lax.axis_index("tm")
    c = lax.axis_index("col")
    o = 1 - c
    pairs = lax.axis_size("tm") // 2
    k = tm // 2
    even = tm % 2 == 0
    odd = tm % 2 == 1
    last = k == pairs - 1
    mate = {"col": o}
    across = {"tm": tm + 1 - 2 * (tm % 2)}

    def copy(which, src, dst, device):
        return pltpu.make_async_remote_copy(
            src_ref=src, dst_ref=dst, send_sem=send.at[which], recv_sem=recv.at[which],
            device_id=device, device_id_type=MESH,
        )

    loads = [
        pltpu.make_async_copy(d_hbm.at[1], d_ref.at[1], load.at[0]),
        pltpu.make_async_copy(h_hbm, h_ref, load.at[1]),
        pltpu.make_async_copy(g_hbm.at[0], g0f.at[c], load.at[2]),
        pltpu.make_async_copy(g_hbm.at[1], g1f.at[c], load.at[3]),
        pltpu.make_async_copy(d_hbm.at[0], d_ref.at[0], load.at[4]),
        pltpu.make_async_copy(a_hbm, a_ref, load.at[5]),
    ]
    for one in loads:
        one.start()

    barrier = pltpu.get_barrier_semaphore()

    def greet(device):
        pl.semaphore_signal(barrier, inc=1, device_id=device, device_id_type=MESH)

    greet(mate)
    greet(across)

    @pl.when(even & (k > 0))
    def _():
        greet({"tm": tm - 2})

    @pl.when(even & jnp.logical_not(last))
    def _():
        greet({"tm": tm + 2})

    loads[0].wait()
    loads[1].wait()
    dh1f[c, :rows] = d_ref[1].astype(BF16)
    dh1f[c, rows:] = h_ref[1]

    before = jnp.where(even & (k > 0), 1, 0)
    after = jnp.where(even & jnp.logical_not(last), 1, 0)
    pl.semaphore_wait(barrier, 2 + before + after)

    first = [
        copy(DH1, dh1f.at[c], dh1f.at[c], mate),
        copy(G0, g_hbm.at[0], g0f.at[c], mate),
        copy(G1, g_hbm.at[1], g1f.at[c], mate),
    ]
    for one in first:
        one.start()
    for one in loads[2:]:
        one.wait()
    first[0].wait_recv()

    def times(left, span, right):
        return mm(jnp.concatenate([left[0, span], left[1, span]], axis=1), right)

    body = pl.ds(0, rows)
    whole = pl.ds(0, tall)

    mine = pl.ds(pl.multiple_of(c * wide, wide), wide)
    other = pl.ds(pl.multiple_of(o * wide, wide), wide)
    first_rows = early + 2 * edge_rows

    def pack_first(p, edge):
        r = pl.multiple_of(c * wide, wide)
        zs[:half] = p[pl.ds(r, half), :half].astype(BF16)
        zs[half : 2 * half] = p[pl.ds(r + half, half), half:].astype(BF16)
        zs[2 * half : early] = p[pl.ds(r, half), half:].astype(BF16)
        zs[early : early + edge_rows] = edge[:, :half].astype(BF16)
        zs[early + edge_rows : first_rows] = edge[:, half:].astype(BF16)

    def pack_second(p):
        @pl.when(c == 0)
        def _():
            zs[first_rows : first_rows + half] = p[wide : wide + half, :half].astype(BF16)
            zs[first_rows + half :] = p[wide + half :, :half].astype(BF16)

        @pl.when(c == 1)
        def _():
            zs[first_rows : first_rows + half] = p[half:wide, :half].astype(BF16)
            zs[first_rows + half :] = p[half:wide, half:].astype(BF16)

    def unpack_first(z, full):
        for j in range(2):
            base = j * wide
            lo = pl.ds(base, half)
            hi = pl.ds(base + half, half)
            full[lo, lo] = z[j, :half]
            full[hi, hi] = z[j, half : 2 * half]
            inner = z[j, 2 * half : early]
            full[lo, hi] = inner
            full[hi, lo] = inner.T
            for n in range(2):
                full[rows:, pl.ds(base + n * half, half)] = z[
                    j, early + n * edge_rows : early + (n + 1) * edge_rows
                ]

    def unpack_second(z, full):
        for j in range(2):
            near = pl.ds(j * half, half)
            for n in range(2):
                outer = z[j, first_rows + n * half : first_rows + (n + 1) * half]
                far = pl.ds(wide + n * half, half)
                if j == 0:
                    full[far, near] = outer
                    full[near, far] = outer.T
                else:
                    full[near, far] = outer
                    full[far, near] = outer.T

    top = pl.ds(0, first_rows)
    low = pl.ds(first_rows, zs.shape[0] - first_rows)

    def pieces(ids, src, dst, device):
        return [
            copy(ids[0], src.at[top], dst.at[top], device),
            copy(ids[1], src.at[low], dst.at[low], device),
        ]

    own0 = g0f[c]
    w = times(dh1f, whole, own0)
    wb = w[:rows].astype(BF16)
    kappa = w[rows:] - h_ref[0].astype(F32)
    pm0[mine] = d_ref[0, mine] + mt(g0f[c], wb)
    out_p = pieces((XA, XB), zs, zp.at[c], across)

    @pl.when(odd)
    def _():
        pack_first(pm0, kappa)
        out_p[0].start()

    first[1].wait_recv()
    pm0[other] = d_ref[0, other] + mt(g0f[o], wb)

    @pl.when(odd)
    def _():
        pack_second(pm0)
        out_p[1].start()

    first[2].wait_recv()
    gk[c, :rows] = times(g1f, body, own0).astype(BF16)
    gk[c, rows:] = kappa.astype(BF16)
    out_g = copy(XG, gk.at[c], g1cf.at[c], across)

    @pl.when(odd)
    def _():
        out_g.start()

    join = copy(GC, gk.at[c], gk.at[c], mate)
    join.start()
    join.wait_recv()
    for j in range(2):
        t0[pl.ds(j * wide, wide), :] = gk[j, :rows].T
        t1[pl.ds(j * wide, wide), :] = g1f[j].T

    chain = pieces((YA, YB), zs, zy.at[c], {"tm": tm - 2})

    @pl.when(odd)
    def _():
        m0[...] = gk[...]
        m1[:, :rows] = g1f[...]
        m1[:, rows:] = -dh1f[:, rows:]
        pm1[...] = d_ref[1]

    @pl.when(even)
    def _():
        ahead = pieces((XFA, XFB), zp.at[c], zp.at[c], mate)
        for one, two in zip(out_p, ahead):
            one.wait_recv()
            two.start()
        ahead[0].wait_recv()
        unpack_first(zp, p1f)
        ahead[1].wait_recv()
        unpack_second(zp, p1f)
        own = gk[c, :rows]
        w = mm(p1f[...], own)
        wb = w[:rows].astype(BF16)
        kz = w[rows:] + gk[c, rows:].astype(F32)
        m0[c, rows:] = kz.astype(BF16)
        pm0[mine] += mm(t0[mine, :], wb)

        @pl.when(last & (k > 0))
        def _():
            pack_first(pm0, kz)
            chain[0].start()

        pm0[other] += mm(t0[other, :], wb)

        @pl.when(last & (k > 0))
        def _():
            pack_second(pm0)
            chain[1].start()

        w1 = mm(p1f[...], g1f[c])
        wb1 = w1[:rows].astype(BF16)
        m1[c, rows:] = (-(w1[rows:] + h_ref[1].astype(F32))).astype(BF16)
        for j in range(2):
            span = pl.ds(j * wide, wide)
            pm1[span] = d_ref[1, span] + mm(t1[span, :], wb1)
        out_g.wait_recv()
        ahead_g = copy(XGF, g1cf.at[c], g1cf.at[c], mate)
        ahead_g.start()
        ahead_g.wait_recv()
        m0[c, :rows] = times(g1cf, body, own).astype(BF16)
        m0x = copy(M0X, m0.at[c], m0.at[c], mate)
        m0x.start()
        m1[c, :rows] = times(g1cf, body, g1f[c]).astype(BF16)
        m1x = copy(M1X, m1.at[c], m1.at[c], mate)
        m1x.start()
        m0x.wait_recv()
        m1x.wait_recv()
        for j in range(2):
            t0[pl.ds(j * wide, wide), :] = m0[j, :rows].T
            t1[pl.ds(j * wide, wide), :] = m1[j, :rows].T
        for two in ahead:
            two.wait_send()
        ahead_g.wait_send()
        m0x.wait_send()
        m1x.wait_send()

    @pl.when(odd)
    def _():
        for one in out_p:
            one.wait_send()
        out_g.wait_send()

    beside = pieces((OA, OB), zy.at[c], zy.at[c], across)
    inner = pieces((FA, FB), zy.at[c], zy.at[c], mate)

    cov = a_ref[...].astype(BF16)

    def edges(step, sign, m):
        for j in range(2):
            kb[step, j] = sign * mm(yin[rows:], m[j, :rows]) + m[j, rows:].astype(F32)

    @pl.when(last)
    def _():
        yin[...] = jnp.zeros_like(yin)

    def relay(n):
        @pl.when(even)
        def _():
            chain[n].wait_recv()
            inner[n].start()
            beside[n].start()

        @pl.when(odd)
        def _():
            beside[n].wait_recv()
            inner[n].start()

    @pl.when(jnp.logical_not(last))
    def _():
        relay(0)
        inner[0].wait_recv()
        unpack_first(zy, yin)

    edges(0, 1.0, m0)
    edges(1, -1.0, m1)
    for step in range(2):
        kb_edge = mm(cov, kb[step, c].astype(BF16))
        cross_ref[step] = kb_edge

    @pl.when(jnp.logical_not(last))
    def _():
        relay(1)
        inner[1].wait_recv()
        unpack_second(zy, yin)

    def state(m):
        return mm(yin[:rows], m[c, :rows]).astype(BF16)

    def emit(step, p):
        edge = cross_ref[step].astype(BF16)
        for j in range(2):
            span = pl.ds(j * wide, wide)
            out_ref[step, span] = p[span] + mt(kb[step, j].astype(BF16), edge)

    passes = even & (k > 0) & jnp.logical_not(last)
    w = state(m0)
    pm0[mine] += mm(t0[mine, :], w)

    @pl.when(passes)
    def _():
        pack_first(pm0, kb[0, c])
        chain[0].start()

    pm0[other] += mm(t0[other, :], w)

    @pl.when(passes)
    def _():
        pack_second(pm0)
        chain[1].start()

    emit(0, pm0)
    w = state(m1)
    for j in range(2):
        span = pl.ds(j * wide, wide)
        pm1[span] += mm(t1[span, :], w)
    emit(1, pm1)
    for one in first:
        one.wait_send()
    join.wait_send()

    @pl.when(jnp.logical_not(last))
    def _():
        for one in inner:
            one.wait_send()

    @pl.when(even & jnp.logical_not(last))
    def _():
        for one in beside:
            one.wait_send()

    @pl.when(even & (k > 0))
    def _():
        for one in chain:
            one.wait_send()


def shards(diagonal_block_inverse, step_map, arrow_map, arrow_cov):
    count, nodes, wide = diagonal_block_inverse.shape
    effects = arrow_map.shape[1]
    tall = nodes + effects
    packed = 5 * (wide // 2) + 2 * effects
    vmem = pl.BlockSpec(memory_space=pltpu.VMEM)
    return pl.pallas_call(
        kernel,
        out_shape=(
            jax.ShapeDtypeStruct((count, nodes, wide), F32),
            jax.ShapeDtypeStruct((count, effects, wide), F32),
        ),
        in_specs=[pl.BlockSpec(memory_space=pltpu.HBM)] * 4,
        out_specs=(vmem, vmem),
        scratch_shapes=[
            pltpu.VMEM((count, nodes, wide), F32),
            pltpu.VMEM((count, effects, wide), BF16),
            pltpu.VMEM((effects, effects), F32),
            pltpu.VMEM((2, nodes, wide), BF16),
            pltpu.VMEM((2, nodes, wide), BF16),
            pltpu.VMEM((2, tall, wide), BF16),
            pltpu.VMEM((2, tall, wide), BF16),
            pltpu.VMEM((nodes, nodes), BF16),
            pltpu.VMEM((nodes, nodes), BF16),
            pltpu.VMEM((packed, wide // 2), BF16),
            pltpu.VMEM((2, packed, wide // 2), BF16),
            pltpu.VMEM((2, packed, wide // 2), BF16),
            pltpu.VMEM((tall, nodes), BF16),
            pltpu.VMEM((2, tall, wide), BF16),
            pltpu.VMEM((2, tall, wide), BF16),
            pltpu.VMEM((2, tall, wide), BF16),
            pltpu.VMEM((nodes, wide), F32),
            pltpu.VMEM((nodes, wide), F32),
            pltpu.VMEM((tall, nodes), BF16),
            pltpu.VMEM((count, 2, effects, wide), F32),
            pltpu.SemaphoreType.DMA((COPIES,)),
            pltpu.SemaphoreType.DMA((COPIES,)),
            pltpu.SemaphoreType.DMA((6,)),
        ],
        compiler_params=pltpu.CompilerParams(
            collective_id=0, has_side_effects=True, vmem_limit_bytes=48 * 1024 * 1024
        ),
    )(diagonal_block_inverse, step_map, arrow_map, arrow_cov)


def solution(mesh):
    return jax.shard_map(
        shards,
        mesh=mesh,
        in_specs=(
            P(("rep", "tm"), None, "col"),
            P(("rep", "tm"), None, "col"),
            P(("rep", "tm"), None, "col"),
            P("rep", None),
        ),
        out_specs=(P(("rep", "tm"), None, "col"), P(("rep", "tm"), None, "col")),
        check_vma=False,
    )
```

```python
import functools
import jax
import jax.numpy as jnp
from jax import lax
from jax.experimental import pallas as pl
from jax.experimental.pallas import tpu as pltpu
from jax.sharding import PartitionSpec as P

MESH = pl.DeviceIdType.MESH
F32 = jnp.float32
BF16 = jnp.bfloat16
G0, G1, DH1, GC, XA, XB, XFA, XFB, XG, XGF, M1X, M0X, YA, YB, OA, OB, FA, FB = range(18)
COPIES = 18


def mm(left, right):
    return jnp.dot(left, right, preferred_element_type=F32)


def mt(left, right):
    return lax.dot_general(left, right, (((0,), (0,)), ((), ())), preferred_element_type=F32)


def kernel(
    d_hbm, g_hbm, h_hbm, a_hbm, out_ref, cross_ref,
    d_ref, h_ref, a_ref, g0f, g1f, dh1f, gk, t0, t1, zs, zp, zy, p1f, g1cf, m1, m0, pm1, pm0,
    yin, kb, send, recv, load,
):
    rows = g0f.shape[1]
    wide = g0f.shape[2]
    tall = gk.shape[1]
    half = wide // 2
    early = 3 * half
    edge_rows = tall - rows
    tm = lax.axis_index("tm")
    c = lax.axis_index("col")
    o = 1 - c
    pairs = lax.axis_size("tm") // 2
    k = tm // 2
    even = tm % 2 == 0
    odd = tm % 2 == 1
    last = k == pairs - 1
    mate = {"col": o}
    across = {"tm": tm + 1 - 2 * (tm % 2)}

    def copy(which, src, dst, device):
        return pltpu.make_async_remote_copy(
            src_ref=src, dst_ref=dst, send_sem=send.at[which], recv_sem=recv.at[which],
            device_id=device, device_id_type=MESH,
        )

    loads = [
        pltpu.make_async_copy(d_hbm.at[1], d_ref.at[1], load.at[0]),
        pltpu.make_async_copy(h_hbm, h_ref, load.at[1]),
        pltpu.make_async_copy(g_hbm.at[0], g0f.at[c], load.at[2]),
        pltpu.make_async_copy(g_hbm.at[1], g1f.at[c], load.at[3]),
        pltpu.make_async_copy(d_hbm.at[0], d_ref.at[0], load.at[4]),
        pltpu.make_async_copy(a_hbm, a_ref, load.at[5]),
    ]
    for one in loads:
        one.start()

    barrier = pltpu.get_barrier_semaphore()

    def greet(device):
        pl.semaphore_signal(barrier, inc=1, device_id=device, device_id_type=MESH)

    greet(mate)
    greet(across)

    @pl.when(even & (k > 0))
    def _():
        greet({"tm": tm - 2})

    @pl.when(even & jnp.logical_not(last))
    def _():
        greet({"tm": tm + 2})

    loads[0].wait()
    loads[1].wait()
    dh1f[c, :rows] = d_ref[1].astype(BF16)
    dh1f[c, rows:] = h_ref[1]

    before = jnp.where(even & (k > 0), 1, 0)
    after = jnp.where(even & jnp.logical_not(last), 1, 0)
    pl.semaphore_wait(barrier, 2 + before + after)

    first = [
        copy(DH1, dh1f.at[c], dh1f.at[c], mate),
        copy(G0, g_hbm.at[0], g0f.at[c], mate),
        copy(G1, g_hbm.at[1], g1f.at[c], mate),
    ]
    for one in first:
        one.start()
    for one in loads[2:]:
        one.wait()
    first[0].wait_recv()

    def times(left, span, right):
        return mm(jnp.concatenate([left[0, span], left[1, span]], axis=1), right)

    body = pl.ds(0, rows)
    whole = pl.ds(0, tall)

    mine = pl.ds(pl.multiple_of(c * wide, wide), wide)
    other = pl.ds(pl.multiple_of(o * wide, wide), wide)
    first_rows = early + 2 * edge_rows

    def pack_first(p, edge):
        r = pl.multiple_of(c * wide, wide)
        zs[:half] = p[pl.ds(r, half), :half].astype(BF16)
        zs[half : 2 * half] = p[pl.ds(r + half, half), half:].astype(BF16)
        zs[2 * half : early] = p[pl.ds(r, half), half:].astype(BF16)
        zs[early : early + edge_rows] = edge[:, :half].astype(BF16)
        zs[early + edge_rows : first_rows] = edge[:, half:].astype(BF16)

    def pack_second(p):
        @pl.when(c == 0)
        def _():
            zs[first_rows : first_rows + half] = p[wide : wide + half, :half].astype(BF16)
            zs[first_rows + half :] = p[wide + half :, :half].astype(BF16)

        @pl.when(c == 1)
        def _():
            zs[first_rows : first_rows + half] = p[half:wide, :half].astype(BF16)
            zs[first_rows + half :] = p[half:wide, half:].astype(BF16)

    def unpack_first(z, full):
        for j in range(2):
            base = j * wide
            lo = pl.ds(base, half)
            hi = pl.ds(base + half, half)
            full[lo, lo] = z[j, :half]
            full[hi, hi] = z[j, half : 2 * half]
            inner = z[j, 2 * half : early]
            full[lo, hi] = inner
            full[hi, lo] = inner.T
            for n in range(2):
                full[rows:, pl.ds(base + n * half, half)] = z[
                    j, early + n * edge_rows : early + (n + 1) * edge_rows
                ]

    def unpack_second(z, full):
        for j in range(2):
            near = pl.ds(j * half, half)
            for n in range(2):
                outer = z[j, first_rows + n * half : first_rows + (n + 1) * half]
                far = pl.ds(wide + n * half, half)
                if j == 0:
                    full[far, near] = outer
                    full[near, far] = outer.T
                else:
                    full[near, far] = outer
                    full[far, near] = outer.T

    top = pl.ds(0, first_rows)
    low = pl.ds(first_rows, zs.shape[0] - first_rows)

    def pieces(ids, src, dst, device):
        return [
            copy(ids[0], src.at[top], dst.at[top], device),
            copy(ids[1], src.at[low], dst.at[low], device),
        ]

    own0 = g0f[c]
    w = times(dh1f, whole, own0)
    wb = w[:rows].astype(BF16)
    kappa = w[rows:] - h_ref[0].astype(F32)
    pm0[mine] = d_ref[0, mine] + mt(g0f[c], wb)
    out_p = pieces((XA, XB), zs, zp.at[c], across)

    @pl.when(odd)
    def _():
        pack_first(pm0, kappa)
        out_p[0].start()

    first[1].wait_recv()
    pm0[other] = d_ref[0, other] + mt(g0f[o], wb)

    @pl.when(odd)
    def _():
        pack_second(pm0)
        out_p[1].start()

    first[2].wait_recv()
    gk[c, :rows] = times(g1f, body, own0).astype(BF16)
    gk[c, rows:] = kappa.astype(BF16)
    out_g = copy(XG, gk.at[c], g1cf.at[c], across)

    @pl.when(odd)
    def _():
        out_g.start()

    join = copy(GC, gk.at[c], gk.at[c], mate)
    join.start()
    join.wait_recv()
    for j in range(2):
        t0[pl.ds(j * wide, wide), :] = gk[j, :rows].T
        t1[pl.ds(j * wide, wide), :] = g1f[j].T

    chain = pieces((YA, YB), zs, zy.at[c], {"tm": tm - 2})

    @pl.when(odd)
    def _():
        m0[...] = gk[...]
        m1[:, :rows] = g1f[...]
        m1[:, rows:] = -dh1f[:, rows:]
        pm1[...] = d_ref[1]

    @pl.when(even)
    def _():
        ahead = pieces((XFA, XFB), zp.at[c], zp.at[c], mate)
        for one, two in zip(out_p, ahead):
            one.wait_recv()
            two.start()
        ahead[0].wait_recv()
        unpack_first(zp, p1f)
        ahead[1].wait_recv()
        unpack_second(zp, p1f)
        own = gk[c, :rows]
        w = mm(p1f[...], own)
        wb = w[:rows].astype(BF16)
        kz = w[rows:] + gk[c, rows:].astype(F32)
        m0[c, rows:] = kz.astype(BF16)
        pm0[mine] += mm(t0[mine, :], wb)

        @pl.when(last & (k > 0))
        def _():
            pack_first(pm0, kz)
            chain[0].start()

        pm0[other] += mm(t0[other, :], wb)

        @pl.when(last & (k > 0))
        def _():
            pack_second(pm0)
            chain[1].start()

        w1 = mm(p1f[...], g1f[c])
        wb1 = w1[:rows].astype(BF16)
        m1[c, rows:] = (-(w1[rows:] + h_ref[1].astype(F32))).astype(BF16)
        for j in range(2):
            span = pl.ds(j * wide, wide)
            pm1[span] = d_ref[1, span] + mm(t1[span, :], wb1)
        out_g.wait_recv()
        ahead_g = copy(XGF, g1cf.at[c], g1cf.at[c], mate)
        ahead_g.start()
        ahead_g.wait_recv()
        m0[c, :rows] = times(g1cf, body, own).astype(BF16)
        m0x = copy(M0X, m0.at[c], m0.at[c], mate)
        m0x.start()
        m1[c, :rows] = times(g1cf, body, g1f[c]).astype(BF16)
        m1x = copy(M1X, m1.at[c], m1.at[c], mate)
        m1x.start()
        m0x.wait_recv()
        m1x.wait_recv()
        for j in range(2):
            t0[pl.ds(j * wide, wide), :] = m0[j, :rows].T
            t1[pl.ds(j * wide, wide), :] = m1[j, :rows].T
        for two in ahead:
            two.wait_send()
        ahead_g.wait_send()
        m0x.wait_send()
        m1x.wait_send()

    @pl.when(odd)
    def _():
        for one in out_p:
            one.wait_send()
        out_g.wait_send()

    beside = pieces((OA, OB), zy.at[c], zy.at[c], across)
    inner = pieces((FA, FB), zy.at[c], zy.at[c], mate)

    cov = a_ref[...].astype(BF16)

    def edges(step, sign, m):
        for j in range(2):
            kb[step, j] = sign * mm(yin[rows:], m[j, :rows]) + m[j, rows:].astype(F32)

    @pl.when(last)
    def _():
        yin[...] = jnp.zeros_like(yin)

    def relay(n):
        @pl.when(even)
        def _():
            chain[n].wait_recv()
            inner[n].start()
            beside[n].start()

        @pl.when(odd)
        def _():
            beside[n].wait_recv()
            inner[n].start()

    @pl.when(jnp.logical_not(last))
    def _():
        relay(0)
        inner[0].wait_recv()
        unpack_first(zy, yin)

    edges(0, 1.0, m0)
    edges(1, -1.0, m1)
    for step in range(2):
        kb_edge = mm(cov, kb[step, c].astype(BF16))
        cross_ref[step] = kb_edge

    @pl.when(jnp.logical_not(last))
    def _():
        relay(1)
        inner[1].wait_recv()
        unpack_second(zy, yin)

    def state(m):
        return mm(yin[:rows], m[c, :rows]).astype(BF16)

    def emit(step, p):
        edge = cross_ref[step].astype(BF16)
        for j in range(2):
            span = pl.ds(j * wide, wide)
            out_ref[step, span] = p[span] + mt(kb[step, j].astype(BF16), edge)

    passes = even & (k > 0) & jnp.logical_not(last)
    w = state(m0)
    pm0[mine] += mm(t0[mine, :], w)

    @pl.when(passes)
    def _():
        pack_first(pm0, kb[0, c])
        chain[0].start()

    pm0[other] += mm(t0[other, :], w)

    @pl.when(passes)
    def _():
        pack_second(pm0)
        chain[1].start()

    emit(0, pm0)
    w = state(m1)
    for j in range(2):
        span = pl.ds(j * wide, wide)
        pm1[span] += mm(t1[span, :], w)
    emit(1, pm1)
    for one in first:
        one.wait_send()
    join.wait_send()

    @pl.when(jnp.logical_not(last))
    def _():
        for one in inner:
            one.wait_send()

    @pl.when(even & jnp.logical_not(last))
    def _():
        for one in beside:
            one.wait_send()

    @pl.when(even & (k > 0))
    def _():
        for one in chain:
            one.wait_send()


def shards(diagonal_block_inverse, step_map, arrow_map, arrow_cov):
    count, nodes, wide = diagonal_block_inverse.shape
    effects = arrow_map.shape[1]
    tall = nodes + effects
    packed = 5 * (wide // 2) + 2 * effects
    vmem = pl.BlockSpec(memory_space=pltpu.VMEM)
    return pl.pallas_call(
        kernel,
        out_shape=(
            jax.ShapeDtypeStruct((count, nodes, wide), F32),
            jax.ShapeDtypeStruct((count, effects, wide), F32),
        ),
        in_specs=[pl.BlockSpec(memory_space=pltpu.HBM)] * 4,
        out_specs=(vmem, vmem),
        scratch_shapes=[
            pltpu.VMEM((count, nodes, wide), F32),
            pltpu.VMEM((count, effects, wide), BF16),
            pltpu.VMEM((effects, effects), F32),
            pltpu.VMEM((2, nodes, wide), BF16),
            pltpu.VMEM((2, nodes, wide), BF16),
            pltpu.VMEM((2, tall, wide), BF16),
            pltpu.VMEM((2, tall, wide), BF16),
            pltpu.VMEM((nodes, nodes), BF16),
            pltpu.VMEM((nodes, nodes), BF16),
            pltpu.VMEM((packed, wide // 2), BF16),
            pltpu.VMEM((2, packed, wide // 2), BF16),
            pltpu.VMEM((2, packed, wide // 2), BF16),
            pltpu.VMEM((tall, nodes), BF16),
            pltpu.VMEM((2, tall, wide), BF16),
            pltpu.VMEM((2, tall, wide), BF16),
            pltpu.VMEM((2, tall, wide), BF16),
            pltpu.VMEM((nodes, wide), F32),
            pltpu.VMEM((nodes, wide), F32),
            pltpu.VMEM((tall, nodes), BF16),
            pltpu.VMEM((count, 2, effects, wide), F32),
            pltpu.SemaphoreType.DMA((COPIES,)),
            pltpu.SemaphoreType.DMA((COPIES,)),
            pltpu.SemaphoreType.DMA((6,)),
        ],
        compiler_params=pltpu.CompilerParams(
            collective_id=0, has_side_effects=True, vmem_limit_bytes=63 * 1024 * 1024
        ),
    )(diagonal_block_inverse, step_map, arrow_map, arrow_cov)


def solution(mesh):
    return jax.shard_map(
        shards,
        mesh=mesh,
        in_specs=(
            P(("rep", "tm"), None, "col"),
            P(("rep", "tm"), None, "col"),
            P(("rep", "tm"), None, "col"),
            P("rep", None),
        ),
        out_specs=(P(("rep", "tm"), None, "col"), P(("rep", "tm"), None, "col")),
        check_vma=False,
    )
```

```python
import functools
import jax
import jax.numpy as jnp
from jax import lax
from jax.experimental import pallas as pl
from jax.experimental.pallas import tpu as pltpu
from jax.sharding import PartitionSpec as P

MESH = pl.DeviceIdType.MESH
F32 = jnp.float32
BF16 = jnp.bfloat16
G0, G1, DH1, GC, XA, XB, XFA, XFB, XG, XGF, M1X, M0X, YA, YB, OA, OB, FA, FB, QA, QB, QG, QFA, QFB, QFG, QOA, QOB, QOG, N0, N1, LA, LB = range(31)
COPIES = 31


def mm(left, right):
    return jnp.dot(left, right, preferred_element_type=F32)


def mt(left, right):
    return lax.dot_general(left, right, (((0,), (0,)), ((), ())), preferred_element_type=F32)


def kernel(
    d_hbm, g_hbm, h_hbm, a_hbm, out_ref, cross_ref,
    d_ref, h_ref, a_ref, g0f, g1f, dh1f, gk, t0, t1, zs, zp, zy, p1f, g1cf, m1, m0, pm1, pm0,
    zq, zt, gq, pq, n1, n0,
    yin, kb, send, recv, load,
):
    rows = g0f.shape[1]
    wide = g0f.shape[2]
    tall = gk.shape[1]
    half = wide // 2
    early = 3 * half
    edge_rows = tall - rows
    tm = lax.axis_index("tm")
    c = lax.axis_index("col")
    o = 1 - c
    pairs = lax.axis_size("tm") // 2
    k = tm // 2
    even = tm % 2 == 0
    odd = tm % 2 == 1
    lower = k % 2 == 0
    upper = k % 2 == 1
    last = k >= pairs - 2
    heads = even & lower & (k > 0)
    takes = even & upper & jnp.logical_not(last)
    mate = {"col": o}
    across = {"tm": tm + 1 - 2 * (tm % 2)}

    def copy(which, src, dst, device):
        return pltpu.make_async_remote_copy(
            src_ref=src, dst_ref=dst, send_sem=send.at[which], recv_sem=recv.at[which],
            device_id=device, device_id_type=MESH,
        )

    loads = [
        pltpu.make_async_copy(d_hbm.at[1], d_ref.at[1], load.at[0]),
        pltpu.make_async_copy(h_hbm, h_ref, load.at[1]),
        pltpu.make_async_copy(g_hbm.at[0], g0f.at[c], load.at[2]),
        pltpu.make_async_copy(g_hbm.at[1], g1f.at[c], load.at[3]),
        pltpu.make_async_copy(d_hbm.at[0], d_ref.at[0], load.at[4]),
        pltpu.make_async_copy(a_hbm, a_ref, load.at[5]),
    ]
    for one in loads:
        one.start()

    barrier = pltpu.get_barrier_semaphore()

    def greet(device):
        pl.semaphore_signal(barrier, inc=1, device_id=device, device_id_type=MESH)

    greet(mate)
    greet(across)

    @pl.when(heads)
    def _():
        greet({"tm": tm - 2})

    @pl.when(takes)
    def _():
        greet({"tm": tm + 2})

    @pl.when(even)
    def _():
        greet({"tm": tm + 2 - 4 * (k % 2)})

    loads[0].wait()
    loads[1].wait()
    dh1f[c, :rows] = d_ref[1].astype(BF16)
    dh1f[c, rows:] = h_ref[1]

    linked = jnp.where(even, 1, 0) + jnp.where(heads | takes, 1, 0)
    pl.semaphore_wait(barrier, 2 + linked)

    first = [
        copy(DH1, dh1f.at[c], dh1f.at[c], mate),
        copy(G0, g_hbm.at[0], g0f.at[c], mate),
        copy(G1, g_hbm.at[1], g1f.at[c], mate),
    ]
    for one in first:
        one.start()
    for one in loads[2:]:
        one.wait()
    first[0].wait_recv()

    def times(left, span, right):
        return mm(jnp.concatenate([left[0, span], left[1, span]], axis=1), right)

    body = pl.ds(0, rows)
    whole = pl.ds(0, tall)

    mine = pl.ds(pl.multiple_of(c * wide, wide), wide)
    other = pl.ds(pl.multiple_of(o * wide, wide), wide)
    first_rows = early + 2 * edge_rows

    def pack_first(zs, p, edge):
        r = pl.multiple_of(c * wide, wide)
        zs[:half] = p[pl.ds(r, half), :half].astype(BF16)
        zs[half : 2 * half] = p[pl.ds(r + half, half), half:].astype(BF16)
        zs[2 * half : early] = p[pl.ds(r, half), half:].astype(BF16)
        zs[early : early + edge_rows] = edge[:, :half].astype(BF16)
        zs[early + edge_rows : first_rows] = edge[:, half:].astype(BF16)

    def pack_second(zs, p):
        @pl.when(c == 0)
        def _():
            zs[first_rows : first_rows + half] = p[wide : wide + half, :half].astype(BF16)
            zs[first_rows + half :] = p[wide + half :, :half].astype(BF16)

        @pl.when(c == 1)
        def _():
            zs[first_rows : first_rows + half] = p[half:wide, :half].astype(BF16)
            zs[first_rows + half :] = p[half:wide, half:].astype(BF16)

    def unpack_first(z, full):
        for j in range(2):
            base = j * wide
            lo = pl.ds(base, half)
            hi = pl.ds(base + half, half)
            full[lo, lo] = z[j, :half]
            full[hi, hi] = z[j, half : 2 * half]
            inner = z[j, 2 * half : early]
            full[lo, hi] = inner
            full[hi, lo] = inner.T
            for n in range(2):
                full[rows:, pl.ds(base + n * half, half)] = z[
                    j, early + n * edge_rows : early + (n + 1) * edge_rows
                ]

    def unpack_second(z, full):
        for j in range(2):
            near = pl.ds(j * half, half)
            for n in range(2):
                outer = z[j, first_rows + n * half : first_rows + (n + 1) * half]
                far = pl.ds(wide + n * half, half)
                if j == 0:
                    full[far, near] = outer
                    full[near, far] = outer.T
                else:
                    full[near, far] = outer
                    full[far, near] = outer.T

    top = pl.ds(0, first_rows)
    low = pl.ds(first_rows, zs.shape[0] - first_rows)

    def pieces(ids, src, dst, device):
        return [
            copy(ids[0], src.at[top], dst.at[top], device),
            copy(ids[1], src.at[low], dst.at[low], device),
        ]

    own0 = g0f[c]
    w = times(dh1f, whole, own0)
    wb = w[:rows].astype(BF16)
    kappa = w[rows:] - h_ref[0].astype(F32)
    pm0[mine] = d_ref[0, mine] + mt(g0f[c], wb)
    out_p = pieces((XA, XB), zs, zp.at[c], across)

    @pl.when(odd)
    def _():
        pack_first(zs, pm0, kappa)
        out_p[0].start()

    first[1].wait_recv()
    pm0[other] = d_ref[0, other] + mt(g0f[o], wb)

    @pl.when(odd)
    def _():
        pack_second(zs, pm0)
        out_p[1].start()

    first[2].wait_recv()
    gk[c, :rows] = times(g1f, body, own0).astype(BF16)
    gk[c, rows:] = kappa.astype(BF16)
    out_g = copy(XG, gk.at[c], g1cf.at[c], across)

    @pl.when(odd)
    def _():
        out_g.start()

    join = copy(GC, gk.at[c], gk.at[c], mate)
    join.start()
    join.wait_recv()
    for j in range(2):
        t0[pl.ds(j * wide, wide), :] = gk[j, :rows].T
        t1[pl.ds(j * wide, wide), :] = g1f[j].T

    chain = pieces((YA, YB), zs, zy.at[c], {"tm": tm - 2})
    pair_up = pieces((QA, QB), zt, zq.at[c], {"tm": tm - 2})
    pair_map = copy(QG, m0.at[c, body], gq.at[c], {"tm": tm - 2})

    @pl.when(odd)
    def _():
        m0[...] = gk[...]
        m1[:, :rows] = g1f[...]
        m1[:, rows:] = -dh1f[:, rows:]
        pm1[...] = d_ref[1]

    @pl.when(even)
    def _():
        ahead = pieces((XFA, XFB), zp.at[c], zp.at[c], mate)
        for one, two in zip(out_p, ahead):
            one.wait_recv()
            two.start()
        ahead[0].wait_recv()
        unpack_first(zp, p1f)
        ahead[1].wait_recv()
        unpack_second(zp, p1f)
        own = gk[c, :rows]
        w = mm(p1f[...], own)
        wb = w[:rows].astype(BF16)
        kz = w[rows:] + gk[c, rows:].astype(F32)
        m0[c, rows:] = kz.astype(BF16)
        pm0[mine] += mm(t0[mine, :], wb)

        @pl.when(upper)
        def _():
            pack_first(zt, pm0, kz)
            pair_up[0].start()

        pm0[other] += mm(t0[other, :], wb)

        @pl.when(upper)
        def _():
            pack_second(zt, pm0)
            pair_up[1].start()

        w1 = mm(p1f[...], g1f[c])
        wb1 = w1[:rows].astype(BF16)
        m1[c, rows:] = (-(w1[rows:] + h_ref[1].astype(F32))).astype(BF16)
        for j in range(2):
            span = pl.ds(j * wide, wide)
            pm1[span] = d_ref[1, span] + mm(t1[span, :], wb1)
        out_g.wait_recv()
        ahead_g = copy(XGF, g1cf.at[c], g1cf.at[c], mate)
        ahead_g.start()
        ahead_g.wait_recv()
        m0[c, :rows] = times(g1cf, body, own).astype(BF16)
        m0x = copy(M0X, m0.at[c], m0.at[c], mate)
        m0x.start()

        @pl.when(upper)
        def _():
            pair_map.start()

        m1[c, :rows] = times(g1cf, body, g1f[c]).astype(BF16)
        m1x = copy(M1X, m1.at[c], m1.at[c], mate)
        m1x.start()
        m0x.wait_recv()
        m1x.wait_recv()
        for j in range(2):
            t0[pl.ds(j * wide, wide), :] = m0[j, :rows].T
            t1[pl.ds(j * wide, wide), :] = m1[j, :rows].T
        for two in ahead:
            two.wait_send()
        ahead_g.wait_send()
        m0x.wait_send()
        m1x.wait_send()

    @pl.when(odd)
    def _():
        for one in out_p:
            one.wait_send()
        out_g.wait_send()

    @pl.when(upper)
    def _():
        n0[...] = m0[...]
        n1[...] = m1[...]

    side_q = pieces((QOA, QOB), zq.at[c], zq.at[c], across)
    mate_q = pieces((QFA, QFB), zq.at[c], zq.at[c], mate)
    side_g = copy(QOG, gq.at[c], gq.at[c], across)
    mate_g = copy(QFG, gq.at[c], gq.at[c], mate)
    grown = [copy(N0, n0.at[c], n0.at[c], mate), copy(N1, n1.at[c], n1.at[c], mate)]

    @pl.when(lower)
    def _():
        for n in range(2):

            @pl.when(even)
            def _():
                pair_up[n].wait_recv()
                mate_q[n].start()
                side_q[n].start()

            @pl.when(odd)
            def _():
                side_q[n].wait_recv()
                mate_q[n].start()

        mate_q[0].wait_recv()
        unpack_first(zq, pq)
        mate_q[1].wait_recv()
        unpack_second(zq, pq)
        w = mm(pq[...], m0[c, :rows])
        wb = w[:rows].astype(BF16)
        kq = w[rows:] + m0[c, rows:].astype(F32)
        n0[c, rows:] = kq.astype(BF16)
        pm0[mine] += mm(t0[mine, :], wb)

        @pl.when(heads & last)
        def _():
            pack_first(zs, pm0, kq)
            chain[0].start()

        pm0[other] += mm(t0[other, :], wb)

        @pl.when(heads & last)
        def _():
            pack_second(zs, pm0)
            chain[1].start()

        w = mm(pq[...], m1[c, :rows])
        wb = w[:rows].astype(BF16)
        n1[c, rows:] = (m1[c, rows:].astype(F32) - w[rows:]).astype(BF16)
        for j in range(2):
            span = pl.ds(j * wide, wide)
            pm1[span] += mm(t1[span, :], wb)

        @pl.when(even)
        def _():
            pair_map.wait_recv()
            mate_g.start()
            side_g.start()

        @pl.when(odd)
        def _():
            side_g.wait_recv()
            mate_g.start()

        mate_g.wait_recv()
        n0[c, :rows] = times(gq, body, m0[c, :rows]).astype(BF16)
        grown[0].start()
        n1[c, :rows] = times(gq, body, m1[c, :rows]).astype(BF16)
        grown[1].start()
        for one in grown:
            one.wait_recv()
        for j in range(2):
            t0[pl.ds(j * wide, wide), :] = n0[j, :rows].T
            t1[pl.ds(j * wide, wide), :] = n1[j, :rows].T
        for one in grown + mate_q:
            one.wait_send()
        mate_g.wait_send()

        @pl.when(even)
        def _():
            for one in side_q:
                one.wait_send()
            side_g.wait_send()

    @pl.when(even & upper)
    def _():
        for one in pair_up:
            one.wait_send()
        pair_map.wait_send()

    below = pieces((LA, LB), zy.at[c], zy.at[c], {"tm": tm - 2})
    beside = pieces((OA, OB), zy.at[c], zy.at[c], across)
    inner = pieces((FA, FB), zy.at[c], zy.at[c], mate)

    cov = a_ref[...].astype(BF16)

    def edges(step, sign, m):
        for j in range(2):
            kb[step, j] = sign * mm(yin[rows:], m[j, :rows]) + m[j, rows:].astype(F32)

    @pl.when(last)
    def _():
        yin[...] = jnp.zeros_like(yin)

    def relay(n):
        @pl.when(even & upper)
        def _():
            chain[n].wait_recv()
            below[n].start()
            inner[n].start()
            beside[n].start()

        @pl.when(even & lower)
        def _():
            below[n].wait_recv()
            inner[n].start()
            beside[n].start()

        @pl.when(odd)
        def _():
            beside[n].wait_recv()
            inner[n].start()

    @pl.when(jnp.logical_not(last))
    def _():
        relay(0)
        inner[0].wait_recv()
        unpack_first(zy, yin)

    edges(0, 1.0, n0)
    edges(1, -1.0, n1)
    for step in range(2):
        kb_edge = mm(cov, kb[step, c].astype(BF16))
        cross_ref[step] = kb_edge

    @pl.when(jnp.logical_not(last))
    def _():
        relay(1)
        inner[1].wait_recv()
        unpack_second(zy, yin)

    def state(m):
        return mm(yin[:rows], m[c, :rows]).astype(BF16)

    def emit(step, p):
        edge = cross_ref[step].astype(BF16)
        for j in range(2):
            span = pl.ds(j * wide, wide)
            out_ref[step, span] = p[span] + mt(kb[step, j].astype(BF16), edge)

    passes = heads & jnp.logical_not(last)
    w = state(n0)
    pm0[mine] += mm(t0[mine, :], w)

    @pl.when(passes)
    def _():
        pack_first(zs, pm0, kb[0, c])
        chain[0].start()

    pm0[other] += mm(t0[other, :], w)

    @pl.when(passes)
    def _():
        pack_second(zs, pm0)
        chain[1].start()

    emit(0, pm0)
    w = state(n1)
    for j in range(2):
        span = pl.ds(j * wide, wide)
        pm1[span] += mm(t1[span, :], w)
    emit(1, pm1)
    for one in first:
        one.wait_send()
    join.wait_send()

    @pl.when(jnp.logical_not(last))
    def _():
        for one in inner:
            one.wait_send()

    @pl.when(even & jnp.logical_not(last))
    def _():
        for one in beside:
            one.wait_send()

    @pl.when(takes)
    def _():
        for one in below:
            one.wait_send()

    @pl.when(heads)
    def _():
        for one in chain:
            one.wait_send()


def shards(diagonal_block_inverse, step_map, arrow_map, arrow_cov):
    count, nodes, wide = diagonal_block_inverse.shape
    effects = arrow_map.shape[1]
    tall = nodes + effects
    packed = 5 * (wide // 2) + 2 * effects
    vmem = pl.BlockSpec(memory_space=pltpu.VMEM)
    return pl.pallas_call(
        kernel,
        out_shape=(
            jax.ShapeDtypeStruct((count, nodes, wide), F32),
            jax.ShapeDtypeStruct((count, effects, wide), F32),
        ),
        in_specs=[pl.BlockSpec(memory_space=pltpu.HBM)] * 4,
        out_specs=(vmem, vmem),
        scratch_shapes=[
            pltpu.VMEM((count, nodes, wide), F32),
            pltpu.VMEM((count, effects, wide), BF16),
            pltpu.VMEM((effects, effects), F32),
            pltpu.VMEM((2, nodes, wide), BF16),
            pltpu.VMEM((2, nodes, wide), BF16),
            pltpu.VMEM((2, tall, wide), BF16),
            pltpu.VMEM((2, tall, wide), BF16),
            pltpu.VMEM((nodes, nodes), BF16),
            pltpu.VMEM((nodes, nodes), BF16),
            pltpu.VMEM((packed, wide // 2), BF16),
            pltpu.VMEM((2, packed, wide // 2), BF16),
            pltpu.VMEM((2, packed, wide // 2), BF16),
            pltpu.VMEM((tall, nodes), BF16),
            pltpu.VMEM((2, tall, wide), BF16),
            pltpu.VMEM((2, tall, wide), BF16),
            pltpu.VMEM((2, tall, wide), BF16),
            pltpu.VMEM((nodes, wide), F32),
            pltpu.VMEM((nodes, wide), F32),
            pltpu.VMEM((2, packed, wide // 2), BF16),
            pltpu.VMEM((packed, wide // 2), BF16),
            pltpu.VMEM((2, nodes, wide), BF16),
            pltpu.VMEM((tall, nodes), BF16),
            pltpu.VMEM((2, tall, wide), BF16),
            pltpu.VMEM((2, tall, wide), BF16),
            pltpu.VMEM((tall, nodes), BF16),
            pltpu.VMEM((count, 2, effects, wide), F32),
            pltpu.SemaphoreType.DMA((COPIES,)),
            pltpu.SemaphoreType.DMA((COPIES,)),
            pltpu.SemaphoreType.DMA((6,)),
        ],
        compiler_params=pltpu.CompilerParams(
            collective_id=0, has_side_effects=True, vmem_limit_bytes=63 * 1024 * 1024
        ),
    )(diagonal_block_inverse, step_map, arrow_map, arrow_cov)


def solution(mesh):
    return jax.shard_map(
        shards,
        mesh=mesh,
        in_specs=(
            P(("rep", "tm"), None, "col"),
            P(("rep", "tm"), None, "col"),
            P(("rep", "tm"), None, "col"),
            P("rep", None),
        ),
        out_specs=(P(("rep", "tm"), None, "col"), P(("rep", "tm"), None, "col")),
        check_vma=False,
    )
```

```python
import functools
import jax
import jax.numpy as jnp
from jax import lax
from jax.experimental import pallas as pl
from jax.experimental.pallas import tpu as pltpu
from jax.sharding import PartitionSpec as P

MESH = pl.DeviceIdType.MESH
F32 = jnp.float32
BF16 = jnp.bfloat16
G0, G1, DH1, GC, XA, XB, XFA, XFB, XG, XGF, M1X, M0X, YA, YB, OA, OB, FA, FB, QA, QB, QG, QFA, QFB, QFG, QOA, QOB, QOG, N0, N1, LA, LB, QG2, QFG2, QOG2 = range(34)
COPIES = 34


def mm(left, right):
    return jnp.dot(left, right, preferred_element_type=F32)


def mt(left, right):
    return lax.dot_general(left, right, (((0,), (0,)), ((), ())), preferred_element_type=F32)


def kernel(
    d_hbm, g_hbm, h_hbm, a_hbm, out_ref, cross_ref,
    d_ref, h_ref, a_ref, g0f, g1f, dh1f, gk, t0, t1, zs, zp, zy, p1f, g1cf, m1, m0, pm1, pm0,
    zq, zt, gq, pq, n1, n0,
    yin, kb, send, recv, load,
):
    rows = g0f.shape[1]
    wide = g0f.shape[2]
    tall = gk.shape[1]
    half = wide // 2
    early = 3 * half
    edge_rows = tall - rows
    tm = lax.axis_index("tm")
    c = lax.axis_index("col")
    o = 1 - c
    pairs = lax.axis_size("tm") // 2
    k = tm // 2
    even = tm % 2 == 0
    odd = tm % 2 == 1
    lower = k % 2 == 0
    upper = k % 2 == 1
    last = k >= pairs - 2
    heads = even & lower & (k > 0)
    takes = even & upper & jnp.logical_not(last)
    mate = {"col": o}
    across = {"tm": tm + 1 - 2 * (tm % 2)}

    def copy(which, src, dst, device):
        return pltpu.make_async_remote_copy(
            src_ref=src, dst_ref=dst, send_sem=send.at[which], recv_sem=recv.at[which],
            device_id=device, device_id_type=MESH,
        )

    loads = [
        pltpu.make_async_copy(d_hbm.at[1], d_ref.at[1], load.at[0]),
        pltpu.make_async_copy(h_hbm, h_ref, load.at[1]),
        pltpu.make_async_copy(g_hbm.at[0], g0f.at[c], load.at[2]),
        pltpu.make_async_copy(g_hbm.at[1], g1f.at[c], load.at[3]),
        pltpu.make_async_copy(d_hbm.at[0], d_ref.at[0], load.at[4]),
        pltpu.make_async_copy(a_hbm, a_ref, load.at[5]),
    ]
    for one in loads:
        one.start()

    barrier = pltpu.get_barrier_semaphore()

    def greet(device):
        pl.semaphore_signal(barrier, inc=1, device_id=device, device_id_type=MESH)

    greet(mate)
    greet(across)

    @pl.when(heads)
    def _():
        greet({"tm": tm - 2})

    @pl.when(takes)
    def _():
        greet({"tm": tm + 2})

    @pl.when(even)
    def _():
        greet({"tm": tm + 2 - 4 * (k % 2)})

    loads[0].wait()
    loads[1].wait()
    dh1f[c, :rows] = d_ref[1].astype(BF16)
    dh1f[c, rows:] = h_ref[1]

    linked = jnp.where(even, 1, 0) + jnp.where(heads | takes, 1, 0)
    pl.semaphore_wait(barrier, 2 + linked)

    first = [
        copy(DH1, dh1f.at[c], dh1f.at[c], mate),
        copy(G0, g_hbm.at[0], g0f.at[c], mate),
        copy(G1, g_hbm.at[1], g1f.at[c], mate),
    ]
    for one in first:
        one.start()
    for one in loads[2:]:
        one.wait()
    first[0].wait_recv()

    def times(left, span, right):
        return mm(jnp.concatenate([left[0, span], left[1, span]], axis=1), right)

    body = pl.ds(0, rows)
    whole = pl.ds(0, tall)

    mine = pl.ds(pl.multiple_of(c * wide, wide), wide)
    other = pl.ds(pl.multiple_of(o * wide, wide), wide)
    first_rows = early + 2 * edge_rows

    def pack_first(zs, p, edge):
        r = pl.multiple_of(c * wide, wide)
        zs[:half] = p[pl.ds(r, half), :half].astype(BF16)
        zs[half : 2 * half] = p[pl.ds(r + half, half), half:].astype(BF16)
        zs[2 * half : early] = p[pl.ds(r, half), half:].astype(BF16)
        zs[early : early + edge_rows] = edge[:, :half].astype(BF16)
        zs[early + edge_rows : first_rows] = edge[:, half:].astype(BF16)

    def pack_second(zs, p):
        @pl.when(c == 0)
        def _():
            zs[first_rows : first_rows + half] = p[wide : wide + half, :half].astype(BF16)
            zs[first_rows + half :] = p[wide + half :, :half].astype(BF16)

        @pl.when(c == 1)
        def _():
            zs[first_rows : first_rows + half] = p[half:wide, :half].astype(BF16)
            zs[first_rows + half :] = p[half:wide, half:].astype(BF16)

    def unpack_first(z, full):
        for j in range(2):
            base = j * wide
            lo = pl.ds(base, half)
            hi = pl.ds(base + half, half)
            full[lo, lo] = z[j, :half]
            full[hi, hi] = z[j, half : 2 * half]
            inner = z[j, 2 * half : early]
            full[lo, hi] = inner
            full[hi, lo] = inner.T
            for n in range(2):
                full[rows:, pl.ds(base + n * half, half)] = z[
                    j, early + n * edge_rows : early + (n + 1) * edge_rows
                ]

    def unpack_second(z, full):
        for j in range(2):
            near = pl.ds(j * half, half)
            for n in range(2):
                outer = z[j, first_rows + n * half : first_rows + (n + 1) * half]
                far = pl.ds(wide + n * half, half)
                if j == 0:
                    full[far, near] = outer
                    full[near, far] = outer.T
                else:
                    full[near, far] = outer
                    full[far, near] = outer.T

    top = pl.ds(0, first_rows)
    low = pl.ds(first_rows, zs.shape[0] - first_rows)

    def pieces(ids, src, dst, device):
        return [
            copy(ids[0], src.at[top], dst.at[top], device),
            copy(ids[1], src.at[low], dst.at[low], device),
        ]

    own0 = g0f[c]
    w = times(dh1f, whole, own0)
    wb = w[:rows].astype(BF16)
    kappa = w[rows:] - h_ref[0].astype(F32)
    pm0[mine] = d_ref[0, mine] + mt(g0f[c], wb)
    out_p = pieces((XA, XB), zs, zp.at[c], across)

    @pl.when(odd)
    def _():
        pack_first(zs, pm0, kappa)
        out_p[0].start()

    first[1].wait_recv()
    pm0[other] = d_ref[0, other] + mt(g0f[o], wb)

    @pl.when(odd)
    def _():
        pack_second(zs, pm0)
        out_p[1].start()

    first[2].wait_recv()
    gk[c, :rows] = times(g1f, body, own0).astype(BF16)
    gk[c, rows:] = kappa.astype(BF16)
    out_g = copy(XG, gk.at[c], g1cf.at[c], across)

    @pl.when(odd)
    def _():
        out_g.start()

    join = copy(GC, gk.at[c], gk.at[c], mate)
    join.start()
    join.wait_recv()
    for j in range(2):
        t0[pl.ds(j * wide, wide), :] = gk[j, :rows].T
        t1[pl.ds(j * wide, wide), :] = g1f[j].T

    chain = pieces((YA, YB), zs, zy.at[c], {"tm": tm - 2})
    pair_up = pieces((QA, QB), zt, zq.at[c], {"tm": tm - 2})
    parts = [pl.ds(0, wide), pl.ds(wide, wide)]

    def halves(ids, src, device):
        return [copy(i, src.at[c, r], gq.at[c, r], device) for i, r in zip(ids, parts)]

    pair_map = halves((QG, QG2), m0, {"tm": tm - 2})

    @pl.when(odd)
    def _():
        m0[...] = gk[...]
        m1[:, :rows] = g1f[...]
        m1[:, rows:] = -dh1f[:, rows:]
        pm1[...] = d_ref[1]

    @pl.when(even)
    def _():
        ahead = pieces((XFA, XFB), zp.at[c], zp.at[c], mate)
        for one, two in zip(out_p, ahead):
            one.wait_recv()
            two.start()
        ahead[0].wait_recv()
        unpack_first(zp, p1f)
        ahead[1].wait_recv()
        unpack_second(zp, p1f)
        own = gk[c, :rows]
        w = mm(p1f[...], own)
        wb = w[:rows].astype(BF16)
        kz = w[rows:] + gk[c, rows:].astype(F32)
        m0[c, rows:] = kz.astype(BF16)
        pm0[mine] += mm(t0[mine, :], wb)

        @pl.when(upper)
        def _():
            pack_first(zt, pm0, kz)
            pair_up[0].start()

        pm0[other] += mm(t0[other, :], wb)

        @pl.when(upper)
        def _():
            pack_second(zt, pm0)
            pair_up[1].start()

        w1 = mm(p1f[...], g1f[c])
        wb1 = w1[:rows].astype(BF16)
        m1[c, rows:] = (-(w1[rows:] + h_ref[1].astype(F32))).astype(BF16)
        for j in range(2):
            span = pl.ds(j * wide, wide)
            pm1[span] = d_ref[1, span] + mm(t1[span, :], wb1)
        out_g.wait_recv()
        ahead_g = copy(XGF, g1cf.at[c], g1cf.at[c], mate)
        ahead_g.start()
        ahead_g.wait_recv()
        m0[c, :rows] = times(g1cf, body, own).astype(BF16)
        m0x = copy(M0X, m0.at[c], m0.at[c], mate)
        m0x.start()

        @pl.when(upper)
        def _():
            for one in pair_map:
                one.start()

        m1[c, :rows] = times(g1cf, body, g1f[c]).astype(BF16)
        m1x = copy(M1X, m1.at[c], m1.at[c], mate)
        m1x.start()
        m0x.wait_recv()
        m1x.wait_recv()
        for j in range(2):
            t0[pl.ds(j * wide, wide), :] = m0[j, :rows].T
            t1[pl.ds(j * wide, wide), :] = m1[j, :rows].T
        for two in ahead:
            two.wait_send()
        ahead_g.wait_send()
        m0x.wait_send()
        m1x.wait_send()

    @pl.when(odd)
    def _():
        for one in out_p:
            one.wait_send()
        out_g.wait_send()

    @pl.when(upper)
    def _():
        n0[...] = m0[...]
        n1[...] = m1[...]

    side_q = pieces((QOA, QOB), zq.at[c], zq.at[c], across)
    mate_q = pieces((QFA, QFB), zq.at[c], zq.at[c], mate)
    side_g = halves((QOG, QOG2), gq, across)
    mate_g = halves((QFG, QFG2), gq, mate)
    grown = [copy(N0, n0.at[c], n0.at[c], mate), copy(N1, n1.at[c], n1.at[c], mate)]

    @pl.when(lower)
    def _():
        for n in range(2):

            @pl.when(even)
            def _():
                pair_up[n].wait_recv()
                mate_q[n].start()
                side_q[n].start()

            @pl.when(odd)
            def _():
                side_q[n].wait_recv()
                mate_q[n].start()

        mate_q[0].wait_recv()
        unpack_first(zq, pq)
        mate_q[1].wait_recv()
        unpack_second(zq, pq)
        w = mm(pq[...], m0[c, :rows])
        wb = w[:rows].astype(BF16)
        kq = w[rows:] + m0[c, rows:].astype(F32)
        n0[c, rows:] = kq.astype(BF16)
        pm0[mine] += mm(t0[mine, :], wb)

        @pl.when(heads & last)
        def _():
            pack_first(zs, pm0, kq)
            chain[0].start()

        pm0[other] += mm(t0[other, :], wb)

        @pl.when(heads & last)
        def _():
            pack_second(zs, pm0)
            chain[1].start()

        w = mm(pq[...], m1[c, :rows])
        wb = w[:rows].astype(BF16)
        n1[c, rows:] = (m1[c, rows:].astype(F32) - w[rows:]).astype(BF16)
        for j in range(2):
            span = pl.ds(j * wide, wide)
            pm1[span] += mm(t1[span, :], wb)

        @pl.when(even)
        def _():
            for n in range(2):
                pair_map[n].wait_recv()
                side_g[n].start()
                mate_g[n].start()

        @pl.when(odd)
        def _():
            for n in range(2):
                side_g[n].wait_recv()
                mate_g[n].start()

        for one in mate_g:
            one.wait_recv()
        n0[c, :rows] = times(gq, body, m0[c, :rows]).astype(BF16)
        grown[0].start()
        n1[c, :rows] = times(gq, body, m1[c, :rows]).astype(BF16)
        grown[1].start()
        for one in grown:
            one.wait_recv()
        for j in range(2):
            t0[pl.ds(j * wide, wide), :] = n0[j, :rows].T
            t1[pl.ds(j * wide, wide), :] = n1[j, :rows].T
        for one in grown + mate_q:
            one.wait_send()
        for one in mate_g:
            one.wait_send()

        @pl.when(even)
        def _():
            for one in side_q:
                one.wait_send()
            for one in side_g:
                one.wait_send()

    @pl.when(even & upper)
    def _():
        for one in pair_up:
            one.wait_send()
        for one in pair_map:
            one.wait_send()

    below = pieces((LA, LB), zy.at[c], zy.at[c], {"tm": tm - 2})
    beside = pieces((OA, OB), zy.at[c], zy.at[c], across)
    inner = pieces((FA, FB), zy.at[c], zy.at[c], mate)

    cov = a_ref[...].astype(BF16)

    def edges(step, sign, m):
        for j in range(2):
            kb[step, j] = sign * mm(yin[rows:], m[j, :rows]) + m[j, rows:].astype(F32)

    @pl.when(last)
    def _():
        yin[...] = jnp.zeros_like(yin)

    def relay(n):
        @pl.when(even & upper)
        def _():
            chain[n].wait_recv()
            below[n].start()
            inner[n].start()
            beside[n].start()

        @pl.when(even & lower)
        def _():
            below[n].wait_recv()
            inner[n].start()
            beside[n].start()

        @pl.when(odd)
        def _():
            beside[n].wait_recv()
            inner[n].start()

    @pl.when(jnp.logical_not(last))
    def _():
        relay(0)
        inner[0].wait_recv()
        unpack_first(zy, yin)

    edges(0, 1.0, n0)
    edges(1, -1.0, n1)
    for step in range(2):
        kb_edge = mm(cov, kb[step, c].astype(BF16))
        cross_ref[step] = kb_edge

    @pl.when(jnp.logical_not(last))
    def _():
        relay(1)
        inner[1].wait_recv()
        unpack_second(zy, yin)

    def state(m):
        return mm(yin[:rows], m[c, :rows]).astype(BF16)

    def emit(step, p):
        edge = cross_ref[step].astype(BF16)
        for j in range(2):
            span = pl.ds(j * wide, wide)
            out_ref[step, span] = p[span] + mt(kb[step, j].astype(BF16), edge)

    passes = heads & jnp.logical_not(last)
    w = state(n0)
    pm0[mine] += mm(t0[mine, :], w)

    @pl.when(passes)
    def _():
        pack_first(zs, pm0, kb[0, c])
        chain[0].start()

    pm0[other] += mm(t0[other, :], w)

    @pl.when(passes)
    def _():
        pack_second(zs, pm0)
        chain[1].start()

    emit(0, pm0)
    w = state(n1)
    for j in range(2):
        span = pl.ds(j * wide, wide)
        pm1[span] += mm(t1[span, :], w)
    emit(1, pm1)
    for one in first:
        one.wait_send()
    join.wait_send()

    @pl.when(jnp.logical_not(last))
    def _():
        for one in inner:
            one.wait_send()

    @pl.when(even & jnp.logical_not(last))
    def _():
        for one in beside:
            one.wait_send()

    @pl.when(takes)
    def _():
        for one in below:
            one.wait_send()

    @pl.when(heads)
    def _():
        for one in chain:
            one.wait_send()


def shards(diagonal_block_inverse, step_map, arrow_map, arrow_cov):
    count, nodes, wide = diagonal_block_inverse.shape
    effects = arrow_map.shape[1]
    tall = nodes + effects
    packed = 5 * (wide // 2) + 2 * effects
    vmem = pl.BlockSpec(memory_space=pltpu.VMEM)
    return pl.pallas_call(
        kernel,
        out_shape=(
            jax.ShapeDtypeStruct((count, nodes, wide), F32),
            jax.ShapeDtypeStruct((count, effects, wide), F32),
        ),
        in_specs=[pl.BlockSpec(memory_space=pltpu.HBM)] * 4,
        out_specs=(vmem, vmem),
        scratch_shapes=[
            pltpu.VMEM((count, nodes, wide), F32),
            pltpu.VMEM((count, effects, wide), BF16),
            pltpu.VMEM((effects, effects), F32),
            pltpu.VMEM((2, nodes, wide), BF16),
            pltpu.VMEM((2, nodes, wide), BF16),
            pltpu.VMEM((2, tall, wide), BF16),
            pltpu.VMEM((2, tall, wide), BF16),
            pltpu.VMEM((nodes, nodes), BF16),
            pltpu.VMEM((nodes, nodes), BF16),
            pltpu.VMEM((packed, wide // 2), BF16),
            pltpu.VMEM((2, packed, wide // 2), BF16),
            pltpu.VMEM((2, packed, wide // 2), BF16),
            pltpu.VMEM((tall, nodes), BF16),
            pltpu.VMEM((2, tall, wide), BF16),
            pltpu.VMEM((2, tall, wide), BF16),
            pltpu.VMEM((2, tall, wide), BF16),
            pltpu.VMEM((nodes, wide), F32),
            pltpu.VMEM((nodes, wide), F32),
            pltpu.VMEM((2, packed, wide // 2), BF16),
            pltpu.VMEM((packed, wide // 2), BF16),
            pltpu.VMEM((2, nodes, wide), BF16),
            pltpu.VMEM((tall, nodes), BF16),
            pltpu.VMEM((2, tall, wide), BF16),
            pltpu.VMEM((2, tall, wide), BF16),
            pltpu.VMEM((tall, nodes), BF16),
            pltpu.VMEM((count, 2, effects, wide), F32),
            pltpu.SemaphoreType.DMA((COPIES,)),
            pltpu.SemaphoreType.DMA((COPIES,)),
            pltpu.SemaphoreType.DMA((6,)),
        ],
        compiler_params=pltpu.CompilerParams(
            collective_id=0, has_side_effects=True, vmem_limit_bytes=63 * 1024 * 1024
        ),
    )(diagonal_block_inverse, step_map, arrow_map, arrow_cov)


def solution(mesh):
    return jax.shard_map(
        shards,
        mesh=mesh,
        in_specs=(
            P(("rep", "tm"), None, "col"),
            P(("rep", "tm"), None, "col"),
            P(("rep", "tm"), None, "col"),
            P("rep", None),
        ),
        out_specs=(P(("rep", "tm"), None, "col"), P(("rep", "tm"), None, "col")),
        check_vma=False,
    )
```
